32 devices in a mesh: grp: 2 (over core), dev: 16 (over z, y, x).
Axes of the slice: x: 2, y: 2, z: 4, core: 2. Of those that a mesh axis runs over, the one named last changes fastest.
Arguments:
- vectors: bfloat16 [32, 2, 384], P(('grp', 'dev')), may hold values from -6 to 6
- kernel: bfloat16 [32, 128, 384], P(None, ('grp', 'dev')), may hold values from -0.0546875 to 0.0546875
- sensor_slot: int32 [32], replicated, may hold values from 0 to 31, each once
- noise_var: float32 [32], P(('grp', 'dev')), may hold values from 0.1 to 1
- smoothing_rate: float32 [128], P(('grp', 'dev')), may hold values from 0.2 to 3
Outputs:
- hessian_vectors: float32 [32, 2, 384], P(('grp', 'dev'))
The draws below stay inside these ranges and needn't reach their ends.
Inputs may be any that keep to these rules, and one draw needn't show every extreme that they name: sensor_slot is a permutation of the 32 sensors: row sensor_slot[s] of vectors, noise_var and hessian_vectors belongs to sensor s.
All inputs are finite; a program needn't handle non-finite values.
Results may differ from the reference program's by a relative error of at most 0.0011.
Values may be sent and summed in bfloat16 or wider, within the bound.
A program may use at most 64 MiB of HBM per device.

```python
import math
import jax
import jax.numpy as jnp
from jax import lax

ACROSS = 4
ALONG = 1
NT = 384
SWEEPS = 2
NS = 32
NPTS = 128
N_GRP = 2
N_DEV = 16


def block_scale(stream_key, extent, pieces, low, largest):
    def one(position, shards_of):
        heights = jax.random.uniform(jax.random.fold_in(jax.random.fold_in(stream_key, 6), position), (shards_of,), jnp.float32, low / len(pieces), largest / len(pieces))
        return jnp.repeat(jnp.exp(heights), extent[position] // shards_of).reshape((-1,) + (1,) * (len(extent) - position - 1))

    level = one(*pieces[0])
    for cut in pieces[1:]:
        level = level * one(*cut)
    return level


def noise(own_key, shape, spread, reach, split=(), kind=jnp.bfloat16):
    array = spread * jax.random.normal(own_key, shape, jnp.float32)
    if split:
        array = array * block_scale(own_key, shape, split, -0.22, 0.18)
    return jnp.clip(array, -reach, reach).astype(kind)


def setup_inputs(seed: int = 0) -> dict:
    splits = jax.random.split(jax.random.key(seed), 6)
    return {
        "vectors": noise(splits[0], (NS, 2, NT), 1.0, 6.0, ((0, 32),)),
        "kernel": noise(splits[1], (NS, NPTS, NT), (NS * NT) ** -0.5, 0.0546875, ((1, 32),)),
        "sensor_slot": jax.random.permutation(splits[2], NS).astype(jnp.int32),
        "noise_var": jnp.clip(jnp.exp(math.log(1.0) - 2.3025851 * jax.random.uniform(splits[3], (NS,), jnp.float32) ** block_scale(splits[3], (NS,), ((0, 32),), -0.2, 0.2)), 0.1, 1.0),
        "smoothing_rate": jnp.clip(jnp.exp(math.log(3.0) - 2.7080502 * jax.random.uniform(splits[4], (NPTS,), jnp.float32) ** block_scale(splits[4], (NPTS,), ((0, 32),), -0.2, 0.2)), 0.2, 3.0),
    }


def reference(vectors, kernel, sensor_slot, noise_var, smoothing_rate):
    values = vectors.astype(jnp.float32)
    by_sensor = values[sensor_slot]
    fft_length = 2 * NT
    block_size = ACROSS * ALONG
    block_count = N_GRP * N_DEV
    spectra = jnp.fft.rfft(by_sensor, n=fft_length, axis=-1)

    def correlate(block_index):
        first_point = (block_index * block_size).astype(jnp.int32)
        kernel_block = lax.dynamic_slice_in_dim(kernel, first_point, block_size, 1).astype(jnp.float32)
        kernel_hat = jnp.fft.rfft(kernel_block, n=fft_length, axis=-1)
        param_hat = jnp.einsum("skf,svf->kvf", jnp.conj(kernel_hat), spectra)
        return jnp.fft.irfft(param_hat, n=fft_length, axis=-1)[..., :NT]

    params = lax.map(correlate, jnp.arange(block_count, dtype=jnp.int32))
    region_grid = params.reshape(N_GRP, N_DEV, ACROSS, ALONG, 2, NT).transpose(0, 2, 1, 3, 4, 5)
    region_grid = region_grid.reshape(N_GRP, ACROSS, N_DEV * ALONG, 2, NT)
    rate_field = smoothing_rate.reshape(N_GRP, N_DEV, ACROSS, ALONG).transpose(0, 2, 1, 3)
    rate_field = rate_field.reshape(N_GRP, ACROSS, N_DEV * ALONG)[..., None, None]
    for sweep_index in range(SWEEPS):
        padded = jnp.pad(region_grid, ((0, 0), (1, 1), (1, 1), (0, 0), (0, 0)))
        neighbours = padded[:, 1:-1, 2:] + padded[:, 1:-1, :-2] + padded[:, 2:, 1:-1] + padded[:, :-2, 1:-1]
        region_grid = (region_grid + rate_field * neighbours) / (1.0 + 4.0 * rate_field)
    rounded = region_grid.astype(jnp.bfloat16).reshape(N_GRP, ACROSS, N_DEV, ALONG, 2, NT)
    rounded = rounded.transpose(0, 2, 1, 3, 4, 5).reshape(block_count, block_size, 2, NT)

    def convolve(block_index, running_sum):
        first_point = (block_index * block_size).astype(jnp.int32)
        kernel_block = lax.dynamic_slice_in_dim(kernel, first_point, block_size, 1).astype(jnp.float32)
        kernel_hat = jnp.fft.rfft(kernel_block, n=fft_length, axis=-1)
        source_block = lax.dynamic_index_in_dim(rounded, block_index.astype(jnp.int32), 0, keepdims=False)
        source_hat = jnp.fft.rfft(source_block.astype(jnp.float32), n=fft_length, axis=-1)
        data_hat = jnp.einsum("skf,kvf->svf", kernel_hat, source_hat)
        return running_sum + jnp.fft.irfft(data_hat, n=fft_length, axis=-1)[..., :NT]

    predicted = lax.fori_loop(0, block_count, convolve, jnp.zeros((NS, 2, NT), jnp.float32))
    inverse = jnp.argsort(sensor_slot).astype(jnp.int32)
    return predicted[inverse] + noise_var[:, None, None] * values
```

```python
import functools

import jax
import jax.numpy as jnp
from jax import lax
from jax.experimental import pallas as pl
from jax.experimental.pallas import tpu as pltpu
from jax.sharding import PartitionSpec as P

SWEEPS = 2
LANE = 128
F32 = jnp.float32
BF16 = jnp.bfloat16
MESH = pl.DeviceIdType.MESH


def iota(shape, dim):
    return lax.broadcasted_iota(jnp.int32, shape, dim)


def fold_rows(block):
    width = block.shape[1]
    rows = block.shape[0]
    while rows > 8:
        rows //= 2
        block = block[:rows] + pltpu.roll(block[rows:], width - rows, 1)
    return block


def fold_pair(low, high, step):
    width = low.shape[1]
    clear = (iota(low.shape, 0) & step) == 0
    first = jnp.where(clear, low, pltpu.roll(high, step, 0))
    second = jnp.where(clear, pltpu.roll(low, 8 - step, 0), high)
    return first + pltpu.roll(second, width - step, 1)


def spread_rows(row):
    block = jnp.broadcast_to(row, (8, row.shape[1]))
    for step in (4, 2, 1):
        block = jnp.where((iota(block.shape, 0) & step) == 0, block, pltpu.roll(block, step, 1))
    rows = 8
    while rows < LANE:
        block = jnp.concatenate([block, pltpu.roll(block, rows, 1)], axis=0)
        rows *= 2
    return block


def kernel_body(
    n_grp, n_dev, vec_ref, ker_hbm, slot_ref, noise_ref, rate_ref, out_ref,
    ker, gath, rates, halo_own, halo, scat_own, scat, kx_ref, kxt_ref,
    ker_sem, gath_send, gath_recv, rate_send, rate_recv, halo_send, halo_recv, scat_send, scat_recv,
):
    n = n_grp * n_dev
    sensors, points, nt = ker_hbm.shape
    vecs = vec_ref.shape[1]
    chunks = nt // LANE
    pieces = vecs * chunks
    grp, dev = lax.axis_index("grp"), lax.axis_index("dev")
    me = grp * n_dev + dev

    def place(rank):
        return (rank // n_dev, rank % n_dev)

    barrier = pltpu.get_barrier_semaphore()

    @pl.loop(1, n)
    def _(k):
        pl.semaphore_signal(barrier, inc=1, device_id=place((me + k) % n), device_id_type=MESH)

    ker_copy = pltpu.make_async_copy(ker_hbm, ker, ker_sem)
    ker_copy.start()
    own = vec_ref[0].astype(F32)
    own_rows = [own[v : v + 1, LANE * c : LANE * (c + 1)] for v in range(vecs) for c in range(chunks)]
    own_tile = jnp.concatenate(own_rows + [jnp.zeros((8 - pieces, LANE), F32)], axis=0)
    gath[0] = own_tile.astype(BF16)
    row_point = iota((8, LANE), 0) // vecs
    rate = jnp.zeros((8, LANE), F32)
    for a in range(points):
        rate = jnp.where(row_point == a, rate_ref[a], rate)
    rates[0] = rate
    pl.semaphore_wait(barrier, n - 1)

    @pl.loop(1, n)
    def _(k):
        pltpu.make_async_remote_copy(
            src_ref=gath.at[0], dst_ref=gath.at[k], send_sem=gath_send, recv_sem=gath_recv,
            device_id=place((me + k) % n), device_id_type=MESH,
        ).start()

    def beside(offset):
        return (grp, (dev + offset + n_dev) % n_dev)

    rate_copies = [
        pltpu.make_async_remote_copy(
            src_ref=rates.at[0], dst_ref=rates.at[1 + i], send_sem=rate_send.at[i], recv_sem=rate_recv.at[i],
            device_id=beside(offset), device_id_type=MESH,
        )
        for i, offset in enumerate((1, -1))
    ]
    for copy in rate_copies:
        copy.start()

    ker_copy.wait()
    owner = (me - iota((n, n), 0) + n) % n
    pick = (jnp.broadcast_to(slot_ref[...].reshape(1, n), (n, n)) == owner).astype(F32).astype(BF16)
    for p in range(points):
        picked = jnp.dot(pick, ker[:, p, :], preferred_element_type=F32)
        for c in range(chunks):
            part = picked[:, LANE * c : LANE * (c + 1)]
            kx_ref[n * c : n * (c + 1), LANE * p : LANE * (p + 1)] = part.astype(BF16)
    kxt_ref[...] = kx_ref[...].astype(F32).T.astype(BF16)

    group = 32
    wanted = iota((pieces * group, 8 * group), 0)
    sel = ((wanted % group) * 8 + wanted // group == iota((pieces * group, 8 * group), 1)).astype(F32).astype(BF16)
    lower = iota((LANE, LANE), 0) <= iota((LANE, LANE), 1)

    pltpu.make_async_copy(gath.at[1:n], gath.at[1:n], gath_recv).wait()
    parts = []
    for g in range(n // group):
        tiles = gath[group * g : group * (g + 1)].astype(F32).reshape(group * 8, LANE).astype(BF16)
        parts.append(jnp.dot(sel, tiles, preferred_element_type=F32).astype(BF16))

    def data(piece):
        return jnp.concatenate([part[group * piece : group * (piece + 1)] for part in parts], axis=0)

    zero = jnp.zeros((n, LANE), BF16)
    rows = [
        jnp.concatenate(
            [data(v * chunks + c + e) if c + e < chunks else zero for v in range(vecs) for e in range(chunks)], axis=1
        )
        for c in range(chunks)
    ]
    shifted = jnp.concatenate(rows, axis=0)
    leaves = []
    for p in range(points):
        products = jnp.dot(kxt_ref[LANE * p : LANE * (p + 1), :], shifted, preferred_element_type=F32)
        for v in range(vecs):
            block = products[:, nt * v : nt * (v + 1)]
            block = jnp.concatenate([jnp.where(lower, block[:, :LANE], 0.0), block[:, LANE:]], axis=1)
            leaves.append(fold_rows(block))
    step = 4
    while step:
        leaves = [fold_pair(leaves[i], leaves[i + step], step) for i in range(step)]
        step //= 2
    field = leaves[0]
    halo_own[...] = field

    offsets = (1, -1, 2, -2)
    halo_copies = [
        pltpu.make_async_remote_copy(
            src_ref=halo_own, dst_ref=halo.at[i], send_sem=halo_send.at[i], recv_sem=halo_recv.at[i],
            device_id=beside(offset), device_id_type=MESH,
        )
        for i, offset in enumerate(offsets)
    ]
    for copy in halo_copies:
        copy.start()
    for copy in rate_copies + halo_copies:
        copy.wait_recv()

    def wide(tile):
        return jnp.concatenate([tile] * chunks, axis=1)

    row = iota((8, nt), 0)

    def sweep(x, left, right, c):
        up = jnp.where(row < vecs, 0.0, pltpu.roll(x, vecs, 0))
        down = jnp.where(row >= 8 - vecs, 0.0, pltpu.roll(x, 8 - vecs, 0))
        return (x + c * (left + right + up + down)) / (1.0 + 4.0 * c)

    left1 = jnp.where(dev >= 1, halo[0], 0.0)
    right1 = jnp.where(dev < n_dev - 1, halo[1], 0.0)
    left2 = jnp.where(dev >= 2, halo[2], 0.0)
    right2 = jnp.where(dev < n_dev - 2, halo[3], 0.0)
    rate_own = wide(rate)
    centre = sweep(field, left1, right1, rate_own)
    left = jnp.where(dev >= 1, sweep(left1, left2, field, wide(rates[1])), 0.0)
    right = jnp.where(dev < n_dev - 1, sweep(right1, field, right2, wide(rates[2])), 0.0)
    smoothed = sweep(centre, left, right, rate_own)
    rounded = smoothed.astype(BF16).astype(F32)

    blocks = []
    for p in range(points):
        across = []
        for v in range(vecs):
            block = spread_rows(rounded[p * vecs + v : p * vecs + v + 1])
            upper = iota((LANE, LANE), 0) <= iota((LANE, LANE), 1)
            across += [jnp.where(upper, block[:, :LANE], 0.0), block[:, LANE:]]
        blocks.append(jnp.concatenate(across, axis=1).astype(BF16))
    lagged = jnp.concatenate(blocks, axis=0)
    sums = jnp.dot(kx_ref[...], lagged, preferred_element_type=F32)
    for v in range(vecs):
        for e in range(chunks):
            total = None
            for c in range(e + 1):
                first = nt * v + LANE * (e - c)
                term = sums[n * c : n * (c + 1), first : first + LANE]
                total = term if total is None else total + term
            scat_own[:, v * chunks + e, :] = total
    scat_own[:, pieces:, :] = jnp.zeros((n, 8 - pieces, LANE), F32)

    @pl.loop(1, n)
    def _(k):
        pltpu.make_async_remote_copy(
            src_ref=scat_own.at[k], dst_ref=scat.at[k], send_sem=scat_send, recv_sem=scat_recv,
            device_id=place((me - k + n) % n), device_id_type=MESH,
        ).start()

    acc = scat_own[0] + noise_ref[0] * own_tile
    pltpu.make_async_copy(scat.at[1:n], scat.at[1:n], scat_recv).wait()
    acc = acc + jnp.sum(scat[1:n], axis=0)
    for v in range(vecs):
        for c in range(chunks):
            out_ref[0, v : v + 1, LANE * c : LANE * (c + 1)] = acc[v * chunks + c : v * chunks + c + 1]
    for copy in rate_copies + halo_copies:
        copy.wait_send()
    pltpu.make_async_copy(gath.at[1:n], gath.at[1:n], gath_send).wait()
    pltpu.make_async_copy(scat.at[1:n], scat.at[1:n], scat_send).wait()


def solution(mesh):
    n_grp, n_dev = mesh.shape["grp"], mesh.shape["dev"]
    n = n_grp * n_dev

    def body(vectors, kernel, sensor_slot, noise_var, smoothing_rate):
        own, vecs, nt = vectors.shape
        sensors, points, _ = kernel.shape
        chunks = nt // LANE
        vmem, smem = pltpu.VMEM, pltpu.SMEM
        dma = pltpu.SemaphoreType.DMA
        return pl.pallas_call(
            functools.partial(kernel_body, n_grp, n_dev),
            out_shape=jax.ShapeDtypeStruct((own, vecs, nt), F32),
            in_specs=[
                pl.BlockSpec(memory_space=vmem),
                pl.BlockSpec(memory_space=pl.ANY),
                pl.BlockSpec(memory_space=vmem),
                pl.BlockSpec(memory_space=smem),
                pl.BlockSpec(memory_space=smem),
            ],
            out_specs=pl.BlockSpec(memory_space=vmem),
            scratch_shapes=[
                vmem((sensors, points, nt), BF16),
                vmem((n, 8, LANE), BF16),
                vmem((3, 8, LANE), F32),
                vmem((8, nt), F32),
                vmem((4, 8, nt), F32),
                vmem((n, 8, LANE), F32),
                vmem((n, 8, LANE), F32),
                vmem((chunks * n, points * LANE), BF16),
                vmem((points * LANE, chunks * n), BF16),
                dma, dma, dma, dma((2,)), dma((2,)), dma((4,)), dma((4,)), dma, dma,
            ],
            compiler_params=pltpu.CompilerParams(collective_id=0, has_side_effects=True),
        )(vectors, kernel, sensor_slot, noise_var, smoothing_rate)

    return jax.shard_map(
        body,
        mesh=mesh,
        in_specs=(
            P(("grp", "dev"), None, None),
            P(None, ("grp", "dev"), None),
            P(),
            P(("grp", "dev")),
            P(("grp", "dev")),
        ),
        out_specs=P(("grp", "dev"), None, None),
        check_vma=False,
    )
```

```python
import functools

import jax
import jax.numpy as jnp
from jax import lax
from jax.experimental import pallas as pl
from jax.experimental.pallas import tpu as pltpu
from jax.sharding import PartitionSpec as P

SWEEPS = 2
LANE = 128
F32 = jnp.float32
BF16 = jnp.bfloat16
MESH = pl.DeviceIdType.MESH


def iota(shape, dim):
    return lax.broadcasted_iota(jnp.int32, shape, dim)


def fold_rows(block):
    width = block.shape[1]
    rows = block.shape[0]
    while rows > 8:
        rows //= 2
        block = block[:rows] + pltpu.roll(block[rows:], width - rows, 1)
    return block


def fold_pair(low, high, step):
    width = low.shape[1]
    clear = (iota(low.shape, 0) & step) == 0
    first = jnp.where(clear, low, pltpu.roll(high, step, 0))
    second = jnp.where(clear, pltpu.roll(low, 8 - step, 0), high)
    return first + pltpu.roll(second, width - step, 1)


def spread_rows(row):
    block = jnp.broadcast_to(row, (8, row.shape[1]))
    for step in (4, 2, 1):
        block = jnp.where((iota(block.shape, 0) & step) == 0, block, pltpu.roll(block, step, 1))
    rows = 8
    while rows < LANE:
        block = jnp.concatenate([block, pltpu.roll(block, rows, 1)], axis=0)
        rows *= 2
    return block


def kernel_body(
    n_grp, n_dev, vec_hbm, ker_hbm, slot_hbm, noise_hbm, rate_hbm, out_ref,
    vec_ref, slot_ref, noise_ref, rate_ref,    ker, gath, rates, halo_own, halo, scat_own, scat, kx_ref, kxt_ref,
    load_sem, ker_sem, gath_send, gath_recv, rate_send, rate_recv, halo_send, halo_recv, scat_send, scat_recv,
):
    n = n_grp * n_dev
    sensors, points, nt = ker_hbm.shape
    vecs = vec_hbm.shape[1]
    chunks = nt // LANE
    pieces = vecs * chunks
    grp, dev = lax.axis_index("grp"), lax.axis_index("dev")

    def ahead(k):
        return ((grp + k // n_dev) % n_grp, (dev + k % n_dev) % n_dev)

    def behind(k):
        return ((grp - k // n_dev + n_grp) % n_grp, (dev - k % n_dev + n_dev) % n_dev)

    def slot_of(i):
        q = i // n_grp
        along = (n_dev // 2 + (1 - 2 * (q % 2)) * ((q + 1) // 2) + n_dev) % n_dev
        return (n_grp - 1 - i % n_grp) * n_dev + along

    gath[...] = jnp.zeros(gath.shape, BF16)
    barrier = pltpu.get_barrier_semaphore()

    @pl.loop(1, n)
    def _(k):
        pl.semaphore_signal(barrier, inc=1, device_id=ahead(k), device_id_type=MESH)

    loads = [
        pltpu.make_async_copy(source, target, load_sem.at[i])
        for i, (source, target) in enumerate(
            ((vec_hbm, vec_ref), (rate_hbm, rate_ref), (slot_hbm, slot_ref), (noise_hbm, noise_ref))
        )
    ]
    for load in loads:
        load.start()
    ker_copy = pltpu.make_async_copy(ker_hbm, ker, ker_sem)
    ker_copy.start()
    for load in loads:
        load.wait()
    own = vec_ref[0].astype(F32)
    own_rows = [own[v : v + 1, LANE * c : LANE * (c + 1)] for v in range(vecs) for c in range(chunks)]
    own_tile = jnp.concatenate(own_rows + [jnp.zeros((8 - pieces, LANE), F32)], axis=0)
    gath[0] = own_tile.astype(BF16)
    row_point = iota((8, LANE), 0) // vecs
    rate = jnp.zeros((8, LANE), F32)
    for a in range(points):
        rate = jnp.where(row_point == a, rate_ref[a], rate)
    rates[0] = rate
    pl.semaphore_wait(barrier, n - 1)

    @pl.loop(1, n)
    def _(k):
        pltpu.make_async_remote_copy(
            src_ref=gath.at[0, :pieces], dst_ref=gath.at[k, :pieces], send_sem=gath_send, recv_sem=gath_recv,
            device_id=ahead(k), device_id_type=MESH,
        ).start()

    def beside(offset):
        return (grp, (dev + offset + n_dev) % n_dev)

    rate_copies = [
        pltpu.make_async_remote_copy(
            src_ref=rates.at[0], dst_ref=rates.at[1 + i], send_sem=rate_send.at[i], recv_sem=rate_recv.at[i],
            device_id=beside(offset), device_id_type=MESH,
        )
        for i, offset in enumerate((1, -1))
    ]
    targets = [dev < n_dev - 1, dev >= 1, dev < n_dev - 2, dev >= 2]
    sources = [dev >= 1, dev < n_dev - 1, dev >= 2, dev < n_dev - 2]
    for copy, target in zip(rate_copies, targets):
        pl.when(target)(copy.start)

    ker_copy.wait()
    owner_grp, owner_dev = behind(iota((n, n), 0))
    owner = owner_grp * n_dev + owner_dev
    pick = (jnp.broadcast_to(slot_ref[...].reshape(1, n), (n, n)) == owner).astype(F32).astype(BF16)
    for p in range(points):
        picked = jnp.dot(pick, ker[:, p, :], preferred_element_type=F32)
        for c in range(chunks):
            part = picked[:, LANE * c : LANE * (c + 1)]
            kx_ref[n * c : n * (c + 1), LANE * p : LANE * (p + 1)] = part.astype(BF16)
    kxt_ref[...] = kx_ref[...].astype(F32).T.astype(BF16)

    group = 32
    wanted = iota((pieces * group, 8 * group), 0)
    sel = ((wanted % group) * 8 + wanted // group == iota((pieces * group, 8 * group), 1)).astype(F32).astype(BF16)
    lower = iota((LANE, LANE), 0) <= iota((LANE, LANE), 1)

    pltpu.make_async_copy(gath.at[1:n, :pieces], gath.at[1:n, :pieces], gath_recv).wait()
    parts = []
    for g in range(n // group):
        tiles = gath[group * g : group * (g + 1)].astype(F32).reshape(group * 8, LANE).astype(BF16)
        parts.append(jnp.dot(sel, tiles, preferred_element_type=F32).astype(BF16))

    def data(piece):
        return jnp.concatenate([part[group * piece : group * (piece + 1)] for part in parts], axis=0)

    zero = jnp.zeros((n, LANE), BF16)
    rows = [
        jnp.concatenate(
            [data(v * chunks + c + e) if c + e < chunks else zero for v in range(vecs) for e in range(chunks)], axis=1
        )
        for c in range(chunks)
    ]
    shifted = jnp.concatenate(rows, axis=0)
    leaves = []
    for p in range(points):
        products = jnp.dot(kxt_ref[LANE * p : LANE * (p + 1), :], shifted, preferred_element_type=F32)
        for v in range(vecs):
            block = products[:, nt * v : nt * (v + 1)]
            block = jnp.concatenate([jnp.where(lower, block[:, :LANE], 0.0), block[:, LANE:]], axis=1)
            leaves.append(fold_rows(block))
    step = 4
    while step:
        leaves = [fold_pair(leaves[i], leaves[i + step], step) for i in range(step)]
        step //= 2
    field = leaves[0]
    halo_own[...] = field

    offsets = (1, -1, 2, -2)
    halo_copies = [
        pltpu.make_async_remote_copy(
            src_ref=halo_own, dst_ref=halo.at[i], send_sem=halo_send.at[i], recv_sem=halo_recv.at[i],
            device_id=beside(offset), device_id_type=MESH,
        )
        for i, offset in enumerate(offsets)
    ]
    for copy, target in zip(halo_copies, targets):
        pl.when(target)(copy.start)
    for copy, source in zip(rate_copies + halo_copies, sources[:2] + sources):
        pl.when(source)(copy.wait_recv)

    def wide(tile):
        return jnp.concatenate([tile] * chunks, axis=1)

    row = iota((8, nt), 0)

    def sweep(x, left, right, c):
        up = jnp.where(row < vecs, 0.0, pltpu.roll(x, vecs, 0))
        down = jnp.where(row >= 8 - vecs, 0.0, pltpu.roll(x, 8 - vecs, 0))
        return (x + c * (left + right + up + down)) / (1.0 + 4.0 * c)

    left1 = jnp.where(dev >= 1, halo[0], 0.0)
    right1 = jnp.where(dev < n_dev - 1, halo[1], 0.0)
    left2 = jnp.where(dev >= 2, halo[2], 0.0)
    right2 = jnp.where(dev < n_dev - 2, halo[3], 0.0)
    rate_own = wide(rate)
    rate_left = jnp.where(dev >= 1, rates[1], 1.0)
    rate_right = jnp.where(dev < n_dev - 1, rates[2], 1.0)
    centre = sweep(field, left1, right1, rate_own)
    left = jnp.where(dev >= 1, sweep(left1, left2, field, wide(rate_left)), 0.0)
    right = jnp.where(dev < n_dev - 1, sweep(right1, field, right2, wide(rate_right)), 0.0)
    smoothed = sweep(centre, left, right, rate_own)
    rounded = smoothed.astype(BF16).astype(F32)

    blocks = []
    for p in range(points):
        across = []
        for v in range(vecs):
            block = spread_rows(rounded[p * vecs + v : p * vecs + v + 1])
            upper = iota((LANE, LANE), 0) <= iota((LANE, LANE), 1)
            across += [jnp.where(upper, block[:, :LANE], 0.0), block[:, LANE:]]
        blocks.append(jnp.concatenate(across, axis=1).astype(BF16))
    lagged = jnp.concatenate(blocks, axis=0)
    sums = jnp.dot(kx_ref[...], lagged, preferred_element_type=F32)
    for v in range(vecs):
        for e in range(chunks):
            total = None
            for c in range(e + 1):
                first = nt * v + LANE * (e - c)
                term = sums[n * c : n * (c + 1), first : first + LANE]
                total = term if total is None else total + term
            scat_own[:, v * chunks + e, :] = total

    @pl.loop(1, n)
    def _(k):
        pltpu.make_async_remote_copy(
            src_ref=scat_own.at[k, :pieces], dst_ref=scat.at[k, :pieces], send_sem=scat_send, recv_sem=scat_recv,
            device_id=behind(k), device_id_type=MESH,
        ).start()

    acc = scat_own[0, :pieces] + noise_ref[...].reshape(1, 1) * own_tile[:pieces]
    pltpu.make_async_copy(scat.at[1:n, :pieces], scat.at[1:n, :pieces], scat_recv).wait()
    acc = acc + jnp.sum(scat[1:n, :pieces], axis=0)
    for v in range(vecs):
        for c in range(chunks):
            out_ref[0, v : v + 1, LANE * c : LANE * (c + 1)] = acc[v * chunks + c : v * chunks + c + 1]
    for copy, target in zip(rate_copies + halo_copies, targets[:2] + targets):
        pl.when(target)(copy.wait_send)
    pltpu.make_async_copy(gath.at[1:n, :pieces], gath.at[1:n, :pieces], gath_send).wait()
    pltpu.make_async_copy(scat.at[1:n, :pieces], scat.at[1:n, :pieces], scat_send).wait()


def solution(mesh):
    n_grp, n_dev = mesh.shape["grp"], mesh.shape["dev"]
    n = n_grp * n_dev

    def body(vectors, kernel, sensor_slot, noise_var, smoothing_rate):
        own, vecs, nt = vectors.shape
        sensors, points, _ = kernel.shape
        chunks = nt // LANE
        vmem, smem = pltpu.VMEM, pltpu.SMEM
        dma = pltpu.SemaphoreType.DMA
        return pl.pallas_call(
            functools.partial(kernel_body, n_grp, n_dev),
            out_shape=vmem((own, vecs, nt), F32),
            in_specs=[pl.BlockSpec(memory_space=pl.ANY)] * 5,
            out_specs=pl.BlockSpec(memory_space=vmem),
            scratch_shapes=[
                vmem(vectors.shape, BF16),
                vmem(sensor_slot.shape, jnp.int32),
                vmem(noise_var.shape, F32),
                smem(smoothing_rate.shape, F32),
                vmem((sensors, points, nt), BF16),
                vmem((n, 8, LANE), BF16),
                vmem((3, 8, LANE), F32),
                vmem((8, nt), F32),
                vmem((4, 8, nt), F32),
                vmem((n, 8, LANE), F32),
                vmem((n, 8, LANE), F32),
                vmem((chunks * n, points * LANE), BF16),
                vmem((points * LANE, chunks * n), BF16),
                dma((4,)), dma, dma, dma, dma((2,)), dma((2,)), dma((4,)), dma((4,)), dma, dma,
            ],
            compiler_params=pltpu.CompilerParams(collective_id=0, has_side_effects=True),
        )(vectors, kernel, sensor_slot, noise_var, smoothing_rate)

    return jax.shard_map(
        body,
        mesh=mesh,
        in_specs=(
            P(("grp", "dev"), None, None),
            P(None, ("grp", "dev"), None),
            P(),
            P(("grp", "dev")),
            P(("grp", "dev")),
        ),
        out_specs=P(("grp", "dev"), None, None),
        check_vma=False,
    )
```

```python
import functools

import jax
import jax.numpy as jnp
from jax import lax
from jax.experimental import pallas as pl
from jax.experimental.pallas import tpu as pltpu
from jax.sharding import PartitionSpec as P

SWEEPS = 2
LANE = 128
F32 = jnp.float32
BF16 = jnp.bfloat16
MESH = pl.DeviceIdType.MESH


def iota(shape, dim):
    return lax.broadcasted_iota(jnp.int32, shape, dim)


def fold_rows(block):
    width = block.shape[1]
    rows = block.shape[0]
    while rows > 8:
        rows //= 2
        block = block[:rows] + pltpu.roll(block[rows:], width - rows, 1)
    return block


def fold_pair(low, high, step):
    width = low.shape[1]
    clear = (iota(low.shape, 0) & step) == 0
    first = jnp.where(clear, low, pltpu.roll(high, step, 0))
    second = jnp.where(clear, pltpu.roll(low, 8 - step, 0), high)
    return first + pltpu.roll(second, width - step, 1)


def spread_rows(row):
    block = jnp.broadcast_to(row, (8, row.shape[1]))
    for step in (4, 2, 1):
        block = jnp.where((iota(block.shape, 0) & step) == 0, block, pltpu.roll(block, step, 1))
    rows = 8
    while rows < LANE:
        block = jnp.concatenate([block, pltpu.roll(block, rows, 1)], axis=0)
        rows *= 2
    return block


def kernel_body(
    n_grp, n_dev, vec_hbm, ker_hbm, slot_hbm, noise_hbm, rate_hbm, out_ref,
    vec_ref, slot_ref, noise_ref, rate_ref,    ker, gath, rates, halo_own, halo, scat_own, scat, kx_ref, kxt_ref,
    load_sem, ker_sem, gath_send, gath_recv, rate_send, rate_recv, halo_send, halo_recv, scat_send, scat_recv,
):
    n = n_grp * n_dev
    sensors, points, nt = ker_hbm.shape
    vecs = vec_hbm.shape[1]
    chunks = nt // LANE
    pieces = vecs * chunks
    grp, dev = lax.axis_index("grp"), lax.axis_index("dev")

    def behind(k):
        return ((grp - k // n_dev + n_grp) % n_grp, (dev - k % n_dev + n_dev) % n_dev)

    def wrapped(i, size):
        return lax.rem(i + size, size)

    def each_slot(send, sign):
        for kg in range(n_grp):
            there = wrapped(grp + sign * kg, n_grp)

            @pl.loop(0 if kg else 1, n_dev, unroll=True)
            def _(kd, kg=kg, there=there):
                send(kg * n_dev + kd, (there, wrapped(dev + sign * kd, n_dev)))

    gath[...] = jnp.zeros(gath.shape, BF16)
    barrier = pltpu.get_barrier_semaphore()

    each_slot(
        lambda k, device: pl.semaphore_signal(barrier, inc=1, device_id=device, device_id_type=MESH), 1
    )

    loads = [
        pltpu.make_async_copy(source, target, load_sem.at[i])
        for i, (source, target) in enumerate(
            ((vec_hbm, vec_ref), (rate_hbm, rate_ref), (slot_hbm, slot_ref), (noise_hbm, noise_ref))
        )
    ]
    for load in loads:
        load.start()
    ker_copy = pltpu.make_async_copy(ker_hbm, ker, ker_sem)
    ker_copy.start()
    for load in loads:
        load.wait()
    own = vec_ref[0].astype(F32)
    own_rows = [own[v : v + 1, LANE * c : LANE * (c + 1)] for v in range(vecs) for c in range(chunks)]
    own_tile = jnp.concatenate(own_rows + [jnp.zeros((8 - pieces, LANE), F32)], axis=0)
    gath[0] = own_tile.astype(BF16)
    row_point = iota((8, LANE), 0) // vecs
    rate = jnp.zeros((8, LANE), F32)
    for a in range(points):
        rate = jnp.where(row_point == a, rate_ref[a], rate)
    rates[0] = rate
    pl.semaphore_wait(barrier, n - 1)

    def send_data(k, device):
        pltpu.make_async_remote_copy(
            src_ref=gath.at[0, :pieces], dst_ref=gath.at[k, :pieces], send_sem=gath_send, recv_sem=gath_recv,
            device_id=device, device_id_type=MESH,
        ).start()

    each_slot(send_data, 1)

    def beside(offset):
        return (grp, (dev + offset + n_dev) % n_dev)

    rate_copies = [
        pltpu.make_async_remote_copy(
            src_ref=rates.at[0], dst_ref=rates.at[1 + i], send_sem=rate_send.at[i], recv_sem=rate_recv.at[i],
            device_id=beside(offset), device_id_type=MESH,
        )
        for i, offset in enumerate((1, -1))
    ]
    targets = [dev < n_dev - 1, dev >= 1, dev < n_dev - 2, dev >= 2]
    sources = [dev >= 1, dev < n_dev - 1, dev >= 2, dev < n_dev - 2]
    for copy, target in zip(rate_copies, targets):
        pl.when(target)(copy.start)

    ker_copy.wait()
    owner_grp, owner_dev = behind(iota((n, n), 0))
    owner = owner_grp * n_dev + owner_dev
    pick = (jnp.broadcast_to(slot_ref[...].reshape(1, n), (n, n)) == owner).astype(F32).astype(BF16)
    for p in range(points):
        picked = jnp.dot(pick, ker[:, p, :], preferred_element_type=F32)
        for c in range(chunks):
            part = picked[:, LANE * c : LANE * (c + 1)]
            kx_ref[n * c : n * (c + 1), LANE * p : LANE * (p + 1)] = part.astype(BF16)
    kxt_ref[...] = kx_ref[...].astype(F32).T.astype(BF16)

    group = 32
    wanted = iota((pieces * group, 8 * group), 0)
    sel = ((wanted % group) * 8 + wanted // group == iota((pieces * group, 8 * group), 1)).astype(F32).astype(BF16)
    lower = iota((LANE, LANE), 0) <= iota((LANE, LANE), 1)

    pltpu.make_async_copy(gath.at[1:n, :pieces], gath.at[1:n, :pieces], gath_recv).wait()
    parts = []
    for g in range(n // group):
        tiles = gath[group * g : group * (g + 1)].astype(F32).reshape(group * 8, LANE).astype(BF16)
        parts.append(jnp.dot(sel, tiles, preferred_element_type=F32).astype(BF16))

    def data(piece):
        return jnp.concatenate([part[group * piece : group * (piece + 1)] for part in parts], axis=0)

    zero = jnp.zeros((n, LANE), BF16)
    rows = [
        jnp.concatenate(
            [data(v * chunks + c + e) if c + e < chunks else zero for v in range(vecs) for e in range(chunks)], axis=1
        )
        for c in range(chunks)
    ]
    shifted = jnp.concatenate(rows, axis=0)
    leaves = []
    for p in range(points):
        products = jnp.dot(kxt_ref[LANE * p : LANE * (p + 1), :], shifted, preferred_element_type=F32)
        for v in range(vecs):
            block = products[:, nt * v : nt * (v + 1)]
            block = jnp.concatenate([jnp.where(lower, block[:, :LANE], 0.0), block[:, LANE:]], axis=1)
            leaves.append(fold_rows(block))
    step = 4
    while step:
        leaves = [fold_pair(leaves[i], leaves[i + step], step) for i in range(step)]
        step //= 2
    field = leaves[0]
    halo_own[...] = field

    offsets = (1, -1, 2, -2)
    halo_copies = [
        pltpu.make_async_remote_copy(
            src_ref=halo_own, dst_ref=halo.at[i], send_sem=halo_send.at[i], recv_sem=halo_recv.at[i],
            device_id=beside(offset), device_id_type=MESH,
        )
        for i, offset in enumerate(offsets)
    ]
    for copy, target in zip(halo_copies, targets):
        pl.when(target)(copy.start)
    for copy, source in zip(rate_copies + halo_copies, sources[:2] + sources):
        pl.when(source)(copy.wait_recv)

    def wide(tile):
        return jnp.concatenate([tile] * chunks, axis=1)

    row = iota((8, nt), 0)

    def sweep(x, left, right, c):
        up = jnp.where(row < vecs, 0.0, pltpu.roll(x, vecs, 0))
        down = jnp.where(row >= 8 - vecs, 0.0, pltpu.roll(x, 8 - vecs, 0))
        return (x + c * (left + right + up + down)) / (1.0 + 4.0 * c)

    left1 = jnp.where(dev >= 1, halo[0], 0.0)
    right1 = jnp.where(dev < n_dev - 1, halo[1], 0.0)
    left2 = jnp.where(dev >= 2, halo[2], 0.0)
    right2 = jnp.where(dev < n_dev - 2, halo[3], 0.0)
    rate_own = wide(rate)
    rate_left = jnp.where(dev >= 1, rates[1], 1.0)
    rate_right = jnp.where(dev < n_dev - 1, rates[2], 1.0)
    centre = sweep(field, left1, right1, rate_own)
    left = jnp.where(dev >= 1, sweep(left1, left2, field, wide(rate_left)), 0.0)
    right = jnp.where(dev < n_dev - 1, sweep(right1, field, right2, wide(rate_right)), 0.0)
    smoothed = sweep(centre, left, right, rate_own)
    rounded = smoothed.astype(BF16).astype(F32)

    blocks = []
    for p in range(points):
        across = []
        for v in range(vecs):
            block = spread_rows(rounded[p * vecs + v : p * vecs + v + 1])
            upper = iota((LANE, LANE), 0) <= iota((LANE, LANE), 1)
            across += [jnp.where(upper, block[:, :LANE], 0.0), block[:, LANE:]]
        blocks.append(jnp.concatenate(across, axis=1).astype(BF16))
    lagged = jnp.concatenate(blocks, axis=0)
    sums = jnp.dot(kx_ref[...], lagged, preferred_element_type=F32)
    for v in range(vecs):
        for e in range(chunks):
            total = None
            for c in range(e + 1):
                first = nt * v + LANE * (e - c)
                term = sums[n * c : n * (c + 1), first : first + LANE]
                total = term if total is None else total + term
            scat_own[:, v * chunks + e, :] = total

    def send_sums(k, device):
        pltpu.make_async_remote_copy(
            src_ref=scat_own.at[k, :pieces], dst_ref=scat.at[k, :pieces], send_sem=scat_send, recv_sem=scat_recv,
            device_id=device, device_id_type=MESH,
        ).start()

    each_slot(send_sums, -1)

    acc = scat_own[0, :pieces] + noise_ref[...].reshape(1, 1) * own_tile[:pieces]
    pltpu.make_async_copy(scat.at[1:n, :pieces], scat.at[1:n, :pieces], scat_recv).wait()
    acc = acc + jnp.sum(scat[1:n, :pieces], axis=0)
    for v in range(vecs):
        for c in range(chunks):
            out_ref[0, v : v + 1, LANE * c : LANE * (c + 1)] = acc[v * chunks + c : v * chunks + c + 1]
    for copy, target in zip(rate_copies + halo_copies, targets[:2] + targets):
        pl.when(target)(copy.wait_send)
    pltpu.make_async_copy(gath.at[1:n, :pieces], gath.at[1:n, :pieces], gath_send).wait()
    pltpu.make_async_copy(scat.at[1:n, :pieces], scat.at[1:n, :pieces], scat_send).wait()


def solution(mesh):
    n_grp, n_dev = mesh.shape["grp"], mesh.shape["dev"]
    n = n_grp * n_dev

    def body(vectors, kernel, sensor_slot, noise_var, smoothing_rate):
        own, vecs, nt = vectors.shape
        sensors, points, _ = kernel.shape
        chunks = nt // LANE
        vmem, smem = pltpu.VMEM, pltpu.SMEM
        dma = pltpu.SemaphoreType.DMA
        return pl.pallas_call(
            functools.partial(kernel_body, n_grp, n_dev),
            out_shape=vmem((own, vecs, nt), F32),
            in_specs=[pl.BlockSpec(memory_space=pl.ANY)] * 5,
            out_specs=pl.BlockSpec(memory_space=vmem),
            scratch_shapes=[
                vmem(vectors.shape, BF16),
                vmem(sensor_slot.shape, jnp.int32),
                vmem(noise_var.shape, F32),
                smem(smoothing_rate.shape, F32),
                vmem((sensors, points, nt), BF16),
                vmem((n, 8, LANE), BF16),
                vmem((3, 8, LANE), F32),
                vmem((8, nt), F32),
                vmem((4, 8, nt), F32),
                vmem((n, 8, LANE), F32),
                vmem((n, 8, LANE), F32),
                vmem((chunks * n, points * LANE), BF16),
                vmem((points * LANE, chunks * n), BF16),
                dma((4,)), dma, dma, dma, dma((2,)), dma((2,)), dma((4,)), dma((4,)), dma, dma,
            ],
            compiler_params=pltpu.CompilerParams(collective_id=0, has_side_effects=True),
        )(vectors, kernel, sensor_slot, noise_var, smoothing_rate)

    return jax.shard_map(
        body,
        mesh=mesh,
        in_specs=(
            P(("grp", "dev"), None, None),
            P(None, ("grp", "dev"), None),
            P(),
            P(("grp", "dev")),
            P(("grp", "dev")),
        ),
        out_specs=P(("grp", "dev"), None, None),
        check_vma=False,
    )
```
